32 devices in a mesh: groups: 2 (over y), genome: 4 (over z), ancestry: 2 (over x), trait: 2 (over core).
Axes of the slice: x: 2, y: 2, z: 4, core: 2. Of those that a mesh axis runs over, the one named last changes fastest.
Arguments:
- zscores: float32 [2, 64, 8192], P('ancestry', 'trait', ('groups', 'genome')), parts along dimension 2
- ld_diag: bfloat16 [2, 8192, 1024], P('ancestry', ('groups', 'genome')), parts along dimension 1, as said below
- ld_next: bfloat16 [2, 8192, 1024], P('ancestry', ('groups', 'genome')), parts along dimension 1
- prior_precision: float32 [2, 2], replicated, as said below
- chrom_cut: int32 [8], P('groups'), parts along dimension 0, may hold values from 0 to 2047
- band_width: int32 [8], P('groups'), parts along dimension 0, may hold values from 512 to 2047
Outputs:
- effect_sizes: float32 [2, 64, 8192], P('ancestry', 'trait', ('groups', 'genome')), parts along dimension 2
The draws below stay inside these ranges and needn't reach their ends.
There are 2 independent parts, one for each index of `groups`. The reference program is written for one: setup_inputs(seed, part) draws one part's arguments, and reference() takes and returns one part's arrays. A program takes and returns all parts, laid end to end along the dimension named above; an argument that names none is the same for every part. Nothing has to cross between parts.
Inputs may be any that keep to these rules, and one draw needn't show every extreme that they name: `chrom_cut`: an entry below 1024 is the offset within its block of the first variant of a new chromosome; 1024 or more means the block holds no chromosome start. `band_width`: LD between two variants counts only when their distance is below the smaller width of their two blocks. `ld_diag`: each 1024 x 1024 diagonal block is symmetric with a positive diagonal. `prior_precision`: symmetric; each diagonal entry exceeds the sum of the magnitudes of the other entries of its row.
All inputs are finite; a program needn't handle non-finite values.
Results may differ from the reference program's by a relative error of at most 0.0025.
Values may be sent and summed in bfloat16 or wider, within the bound.
A program may use at most 64 MiB of HBM per device.

```python
import math
import jax
import jax.numpy as jnp
from jax import lax

BLOCK = 1024
TRAITS = 64
ITERS = 3
ANCESTRIES = 2
BLOCKS = 4
VARIANTS = 4096


def draw_zscores(key, part):
    subkeys = jax.random.split(key, 7)
    rising = 1.0 + 2.0 * jnp.arange(VARIANTS, dtype=jnp.float32) / VARIANTS
    trait_scale = 0.3 * jnp.exp(jax.random.uniform(subkeys[1], (ANCESTRIES, TRAITS, 1), jnp.float32, 0.0, math.log(10.0)))
    variant_scale = 0.3 * jnp.exp(jax.random.uniform(subkeys[2], (1, 1, VARIANTS), jnp.float32, 0.0, math.log(10.0)))
    trend = jnp.arange(BLOCKS, dtype=jnp.float32) / max(BLOCKS - 1, 1)
    mix_block = 0.5 * jax.random.uniform(subkeys[4], (BLOCKS,), jnp.float32, 0.0, 1.0) + 0.5 * trend
    period_block = jnp.exp(jax.random.uniform(subkeys[5], (BLOCKS,), jnp.float32, math.log(16.0), math.log(float(BLOCK))))
    phase_block = jax.random.uniform(subkeys[6], (ANCESTRIES, TRAITS, BLOCKS), jnp.float32, 0.0, 2.0 * math.pi)
    mix_full = jnp.repeat(mix_block, BLOCK)[None, None, :]
    period_full = jnp.repeat(period_block, BLOCK)[None, None, :]
    phase_full = jnp.repeat(phase_block, BLOCK, axis=2)
    position = (jnp.arange(VARIANTS, dtype=jnp.int32) % BLOCK).astype(jnp.float32)[None, None, :]
    smooth = jnp.sin(2.0 * math.pi * position / period_full + phase_full)
    white = jax.random.normal(subkeys[0], (ANCESTRIES, TRAITS, VARIANTS), jnp.float32)
    mixed = mix_full * math.sqrt(2.0) * smooth + jnp.sqrt(1.0 - mix_full * mix_full) * white
    return (mixed * trait_scale * variant_scale * jnp.sqrt(rising)).astype(jnp.float32)


def draw_ld_diag(key, part):
    subkeys = jax.random.split(key, 3)
    raw_vals = jax.random.uniform(subkeys[0], (ANCESTRIES, BLOCKS, BLOCK, BLOCK), jnp.float32, -1.0, 1.0) * (0.56 / math.sqrt(BLOCK))
    symmetric = 0.5 * (raw_vals + jnp.swapaxes(raw_vals, 2, 3))
    identity = jnp.arange(BLOCK)[:, None] == jnp.arange(BLOCK)[None, :]
    offsets = jnp.abs(jnp.arange(BLOCK)[:, None] - jnp.arange(BLOCK)[None, :]).astype(jnp.float32)
    decay = jnp.exp(-offsets / 8.0)
    trend = (jnp.arange(BLOCKS, dtype=jnp.float32) / max(BLOCKS - 1, 1))[None, :, None, None]
    strength = 0.3 * (0.5 * jax.random.uniform(subkeys[2], (ANCESTRIES, BLOCKS, 1, 1), jnp.float32, 0.0, 1.0) + 0.5 * trend)
    diagonal_vals = jnp.exp(jax.random.uniform(subkeys[1], (ANCESTRIES, BLOCKS, BLOCK, 1), jnp.float32, 0.0, math.log(2.0)))
    tiles = jnp.where(identity, diagonal_vals + strength, symmetric + strength * decay)
    return tiles.reshape(ANCESTRIES, VARIANTS, BLOCK).astype(jnp.bfloat16)


def draw_ld_next(key, part):
    raw_vals = jax.random.uniform(key, (ANCESTRIES, VARIANTS, BLOCK), jnp.float32, -1.0, 1.0) * (0.4 / math.sqrt(BLOCK))
    return raw_vals.astype(jnp.bfloat16)


def draw_prior_precision(key, part):
    subkeys = jax.random.split(key, 2)
    raw_vals = jax.random.uniform(subkeys[0], (ANCESTRIES, ANCESTRIES), jnp.float32, -0.5, 0.5)
    identity = jnp.arange(ANCESTRIES)[:, None] == jnp.arange(ANCESTRIES)[None, :]
    off_diag = jnp.where(identity, 0.0, 0.5 * (raw_vals + raw_vals.T))
    diagonal_vals = 0.2 + jnp.sum(jnp.abs(off_diag), axis=1) + jax.random.uniform(subkeys[1], (ANCESTRIES,), jnp.float32, 0.0, 0.5)
    return jnp.where(identity, diagonal_vals[:, None], off_diag).astype(jnp.float32)


def touch_ends(drawn, rng, smallest, top_value):
    longest = drawn.shape.index(max(drawn.shape))
    spots = []
    for shift in (0, 1):
        where = [jax.random.randint(jax.random.fold_in(rng, axis), (), 0, length) for axis, length in enumerate(drawn.shape)]
        where[longest] = (where[longest] + shift) % drawn.shape[longest]
        spots.append(tuple(where))
    return drawn.at[spots[0]].set(smallest).at[spots[1]].set(top_value)


def setup_inputs(seed: int = 0, part: int = 0) -> dict:
    key_list = jax.random.split(jax.random.key(seed), 7)
    own_keys = jax.random.split(jax.random.fold_in(key_list[6], part), 7)
    zscores = draw_zscores(jax.random.fold_in(jax.random.fold_in(key_list[6], part), 71), part)
    ld_diag = draw_ld_diag(jax.random.fold_in(jax.random.fold_in(key_list[6], part), 71), part)
    ld_next = draw_ld_next(jax.random.fold_in(jax.random.fold_in(key_list[6], part), 71), part)
    prior_precision = draw_prior_precision(jax.random.fold_in(key_list[6], 71), part)
    chrom_cut = touch_ends(jax.random.randint(own_keys[4], (BLOCKS,), 0, 2 * BLOCK), jax.random.fold_in(own_keys[4], 1), 0, (2 * BLOCK) - 1).astype(jnp.int32)
    band_width = touch_ends(jax.random.randint(own_keys[5], (BLOCKS,), BLOCK // 2, 2 * BLOCK), jax.random.fold_in(own_keys[5], 1), BLOCK // 2, (2 * BLOCK) - 1).astype(jnp.int32)
    return {"zscores": zscores, "ld_diag": ld_diag, "ld_next": ld_next, "prior_precision": prior_precision, "chrom_cut": chrom_cut, "band_width": band_width}


def block_masks(cut_here, cut_after, width_here, width_after):
    row_ids = jnp.arange(BLOCK, dtype=jnp.int32)[:, None]
    col_ids = jnp.arange(BLOCK, dtype=jnp.int32)[None, :]
    opened = cut_here < BLOCK
    same_chrom = (opened & (row_ids >= cut_here)) == (opened & (col_ids >= cut_here))
    inside = (jnp.abs(row_ids - col_ids) < width_here) & same_chrom
    before_cut = opened & (row_ids < cut_here)
    across = (BLOCK + col_ids - row_ids < jnp.minimum(width_here, width_after)) & jnp.logical_not(before_cut) & (col_ids < cut_after)
    return inside, across


def reference(zscores, ld_diag, ld_next, prior_precision, chrom_cut, band_width):
    tiles_here = ld_diag.reshape(ANCESTRIES, BLOCKS, BLOCK, BLOCK)
    tiles_after = ld_next.reshape(ANCESTRIES, BLOCKS, BLOCK, BLOCK)

    def masked_tiles(block_id):
        following = jnp.minimum(block_id + 1, BLOCKS - 1)
        inside, across = block_masks(chrom_cut[block_id], chrom_cut[following], band_width[block_id], band_width[following])
        here_tile = jnp.where(inside[None], tiles_here[:, block_id].astype(jnp.float32), jnp.float32(0.0))
        after_tile = jnp.where(across[None], tiles_after[:, block_id].astype(jnp.float32), jnp.float32(0.0))
        return here_tile, after_tile

    def apply_operator(direction_bf):
        as_float = direction_bf.astype(jnp.float32)
        blocked = as_float.reshape(ANCESTRIES, TRAITS, BLOCKS, BLOCK)
        padded = jnp.pad(blocked, ((0, 0), (0, 0), (1, 1), (0, 0)))

        def one_block(block_id):
            here_tile, after_tile = masked_tiles(block_id)
            earlier = jnp.maximum(block_id - 1, 0)
            unused, prev_tile = masked_tiles(earlier)
            x_here = padded[:, :, block_id + 1]
            x_after = padded[:, :, block_id + 2]
            x_before = padded[:, :, block_id]
            result = jnp.einsum("atv,avw->atw", x_here, here_tile)
            result = result + jnp.einsum("atw,avw->atv", x_after, after_tile)
            result = result + jnp.einsum("atv,avw->atw", x_before, prev_tile)
            return result

        band_out = lax.map(one_block, jnp.arange(BLOCKS, dtype=jnp.int32))
        band_out = jnp.transpose(band_out, (1, 2, 0, 3)).reshape(ANCESTRIES, TRAITS, VARIANTS)
        coupled = jnp.einsum("ab,btv->atv", prior_precision, as_float, precision=lax.Precision.HIGHEST)
        return band_out + coupled

    diagonal_vals = jnp.diagonal(tiles_here, axis1=2, axis2=3).reshape(ANCESTRIES, VARIANTS).astype(jnp.float32)
    scaling = (1.0 / (diagonal_vals + jnp.diagonal(prior_precision)[:, None]))[:, None, :]
    solution = jnp.zeros(zscores.shape, jnp.float32)
    residual = zscores
    precond = scaling * residual
    direction = precond
    norm_now = jnp.sum(residual * precond, axis=(0, 2))
    for iteration in range(ITERS):
        image_vec = apply_operator(direction.astype(jnp.bfloat16))
        step_len = norm_now / jnp.sum(direction * image_vec, axis=(0, 2))
        solution = solution + step_len[None, :, None] * direction
        if iteration + 1 < ITERS:
            residual = residual - step_len[None, :, None] * image_vec
            precond = scaling * residual
            norm_next = jnp.sum(residual * precond, axis=(0, 2))
            direction = precond + (norm_next / norm_now)[None, :, None] * direction
            norm_now = norm_next
    return solution
```

```python
import functools

import jax
import jax.numpy as jnp
from jax import lax
from jax.experimental import pallas as pl
from jax.experimental.pallas import tpu as pltpu
from jax.sharding import PartitionSpec as P

MESH = pl.DeviceIdType.MESH
COLS = 256
ROWS = 32
LANES = 128
UNROLL_PEERS = 16


def for_each(start, stop, step_fn):
    if stop - start <= UNROLL_PEERS:
        for index in range(start, stop):
            step_fn(index)
    else:
        lax.fori_loop(start, stop, lambda index, carry: (step_fn(index), carry)[1], 0)


def kernel(
    blocks, pops,
    prior, cuts, widths, z_hbm, diag_hbm, next_hbm,
    out_ref,
    zv, dv, nv, scale, p, pb, image, up, anc, carry_out, carry_in, sums, tail,
    load_sem, up_send, up_recv, anc_send, anc_recv, carry_send, carry_recv,
    sums_send, sums_recv, tail_send, tail_recv,
):
    traits, length = zv.shape
    members = blocks * pops
    pos = lax.axis_index("genome")
    pop = lax.axis_index("ancestry")
    before = jnp.maximum(pos - 1, 0)
    after = jnp.minimum(pos + 1, blocks - 1)

    loads = [
        pltpu.make_async_copy(src, dst, load_sem.at[i])
        for i, (src, dst) in enumerate(
            [(z_hbm.at[0], zv), (diag_hbm.at[0], dv), (next_hbm.at[0], nv)]
        )
    ]
    for load in loads:
        load.start()

    def peer(offset):
        return {
            "genome": lax.rem(pos + offset // pops, blocks),
            "ancestry": lax.rem(pop + offset % pops, pops),
        }

    barrier = pltpu.get_barrier_semaphore()
    for_each(
        1, members,
        lambda k: pl.semaphore_signal(barrier, inc=1, device_id=peer(k), device_id_type=MESH),
    )

    def up_copy(k):
        return pltpu.make_async_remote_copy(
            pb.at[k], up.at[k], up_send.at[k], up_recv.at[k],
            device_id={"genome": before}, device_id_type=MESH,
        )

    def carry_copy(k):
        return pltpu.make_async_remote_copy(
            carry_out.at[k], carry_in.at[k], carry_send.at[k], carry_recv.at[k],
            device_id={"genome": after}, device_id_type=MESH,
        )

    def anc_copy(k, shift):
        return pltpu.make_async_remote_copy(
            pb.at[k], anc.at[k, shift - 1], anc_send.at[k, shift - 1], anc_recv.at[k, shift - 1],
            device_id={"ancestry": lax.rem(pop + shift, pops)}, device_id_type=MESH,
        )

    def sums_copy(k):
        return pltpu.make_async_remote_copy(
            sums.at[0], sums.at[k], sums_send.at[k], sums_recv.at[k],
            device_id=peer(k), device_id_type=MESH,
        )

    def tail_copy(k):
        return pltpu.make_async_remote_copy(
            tail.at[0], tail.at[k], tail_send.at[k], tail_recv.at[k],
            device_id=peer(k), device_id_type=MESH,
        )

    has_before = pos > 0
    has_after = pos < blocks - 1

    @pl.when(pos == blocks - 1)
    def _():
        up[...] = jnp.zeros_like(up)

    @pl.when(pos == 0)
    def _():
        carry_in[...] = jnp.zeros_like(carry_in)

    def send_direction(k):
        @pl.when(has_before)
        def _():
            up_copy(k).start()

        for shift in range(1, pops):
            anc_copy(k, shift).start()

    cut_here, cut_after = cuts[pos], cuts[after]
    width_here = widths[pos]
    width_both = jnp.minimum(width_here, widths[after])
    cut_here = jnp.minimum(cut_here, length)
    cut_after = jnp.where(has_after, jnp.minimum(cut_after, length), 0)

    loads[0].wait()
    loads[1].wait()
    self_weight = prior[pop, pop]
    eye = lax.broadcasted_iota(jnp.int32, (LANES, LANES), 0) == lax.broadcasted_iota(
        jnp.int32, (LANES, LANES), 1
    )
    for b in range(length // LANES):
        at = pl.ds(b * LANES, LANES)
        tile = jnp.where(eye, dv[at, at].astype(jnp.float32), 0.0)
        scale[:, at] = 1.0 / (jnp.sum(tile, axis=0, keepdims=True) + self_weight)
    p[0] = scale[...] * zv[...]
    pb[0] = p[0].astype(jnp.bfloat16)

    pl.semaphore_wait(barrier, members - 1)
    send_direction(0)

    col_ids = lax.broadcasted_iota(jnp.int32, (ROWS, length), 1)
    row_base = lax.broadcasted_iota(jnp.int32, (ROWS, 1), 0)

    loads[2].wait()

    def mask_next(i, carry):
        at = pl.ds(pl.multiple_of(i * ROWS, ROWS), ROWS)
        rows = row_base + i * ROWS
        opened = (rows < cut_here) & (cut_here < length)
        high = jnp.minimum(width_both - length + rows, cut_after)
        high = jnp.where(opened, 0, high)
        tile = nv[at, :].astype(jnp.float32)
        nv[at, :] = jnp.where(col_ids < high, tile, 0.0).astype(jnp.bfloat16)
        return carry

    lax.fori_loop(0, length // ROWS, mask_next, 0)

    def send_carry(k):
        for j in range(length // COLS):
            at = pl.ds(j * COLS, COLS)
            carry_out[k, :, at] = jnp.dot(
                pb[k], nv[:, at], preferred_element_type=jnp.float32
            ).astype(jnp.bfloat16)

        @pl.when(has_after)
        def _():
            carry_copy(k).start()

    send_carry(0)

    def mask_diag(i, carry):
        at = pl.ds(pl.multiple_of(i * ROWS, ROWS), ROWS)
        rows = row_base + i * ROWS
        left = rows < cut_here
        low = jnp.maximum(rows - width_here + 1, jnp.where(left, 0, cut_here))
        high = jnp.minimum(rows + width_here, jnp.where(left, cut_here, length))
        tile = dv[at, :].astype(jnp.float32)
        keep = (col_ids >= low) & (col_ids < high)
        dv[at, :] = jnp.where(keep, tile, 0.0).astype(jnp.bfloat16)
        return carry

    lax.fori_loop(0, length // ROWS, mask_diag, 0)

    def dot_diag(k):
        for j in range(length // COLS):
            at = pl.ds(j * COLS, COLS)
            image[k, :, at] = self_weight * pb[k, :, at].astype(jnp.float32) + jnp.dot(
                pb[k], dv[:, at], preferred_element_type=jnp.float32
            )

    def wait_up(k):
        @pl.when(has_after)
        def _():
            up_copy(k).wait_recv()

    def dot_up(k, j):
        at = pl.ds(j * COLS, COLS)
        return lax.dot_general(
            up[k], nv[at, :], (((1,), (1,)), ((), ())), preferred_element_type=jnp.float32
        )

    def coupled(k):
        total = 0.0
        for shift in range(1, pops):
            anc_copy(k, shift).wait_recv()
            other = lax.rem(pop + pops - shift, pops)
            total = total + prior[pop, other] * anc[k, shift - 1].astype(jnp.float32)
        return total

    def inner(left, right):
        return jnp.sum(left * right, axis=1, keepdims=True)

    for k in range(2):
        if k > 0:
            send_direction(k)
            send_carry(k)
        dot_diag(k)
        wait_up(k)
        for j in range(length // COLS):
            at = pl.ds(j * COLS, COLS)
            image[k, :, at] = image[k, :, at] + dot_up(k, j)
        both = image[k] + coupled(k)

        @pl.when(has_before)
        def _():
            carry_copy(k).wait_recv()

        both = both + carry_in[k].astype(jnp.float32)
        image[k] = both
        following = scale[...] * both - p[k]
        p[k + 1] = following
        pb[k + 1] = following.astype(jnp.bfloat16)

    send_direction(2)

    lane_ids = lax.broadcasted_iota(jnp.int32, (traits, LANES), 1)

    def as_rows(columns):
        packed = jnp.zeros((traits, LANES), jnp.float32)
        for j, column in enumerate(columns):
            packed = jnp.where(lane_ids == j, column, packed)
        packed = jnp.concatenate(
            [packed, jnp.zeros((LANES - traits, LANES), jnp.float32)], axis=0
        )
        return jnp.transpose(packed)[:8]

    sums[0] = as_rows([
        inner(p[0], zv[...]), inner(p[1], zv[...]), inner(p[2], zv[...]),
        inner(p[0], image[0]), inner(p[0], image[1]), inner(p[1], image[1]),
        inner(p[2], image[0]), inner(p[2], image[1]),
    ])
    for_each(1, members, lambda k: sums_copy(k).start())

    dot_diag(2)
    wait_up(2)
    for j in range(length // COLS):
        at = pl.ds(j * COLS, COLS)
        image[2, :, at] = image[2, :, at] + 2.0 * dot_up(2, j)
    last = inner(p[2], image[2] + coupled(2))
    tail[0] = as_rows([last])[:1]
    for_each(1, members, lambda k: tail_copy(k).start())

    for_each(1, members, lambda k: sums_copy(k).wait_recv())
    total = jnp.sum(sums[...], axis=0)
    b0, b1, b2, g00, g01, g11, g02, g12 = (total[j : j + 1] for j in range(8))
    l10 = g01 / g00
    d1 = g11 - l10 * g01
    l20 = g02 / g00
    cross = g12 - l20 * g01
    l21 = cross / d1
    y1 = b1 - l10 * b0
    y2 = b2 - l20 * b0 - l21 * y1
    known = l20 * g02 + l21 * cross
    z0 = b0 / g00
    z1 = y1 / d1

    for_each(1, members, lambda k: tail_copy(k).wait_recv())
    g22 = jnp.sum(tail[...], axis=0)
    c2 = y2 / (g22 - known)
    c1 = z1 - l21 * c2
    c0 = z0 - l10 * c1 - l20 * c2
    stacked = jnp.concatenate(
        [c0, c1, c2, jnp.zeros((LANES - 3, LANES), jnp.float32)], axis=0
    )
    stacked = jnp.transpose(stacked)[:traits]
    out_ref[0] = (
        stacked[:, 0:1] * p[0] + stacked[:, 1:2] * p[1] + stacked[:, 2:3] * p[2]
    )

    for k in range(3):
        @pl.when(has_before)
        def _():
            up_copy(k).wait_send()

        for shift in range(1, pops):
            anc_copy(k, shift).wait_send()
    for k in range(2):
        @pl.when(has_after)
        def _():
            carry_copy(k).wait_send()
    for_each(1, members, lambda k: sums_copy(k).wait_send())
    for_each(1, members, lambda k: tail_copy(k).wait_send())


def solution(mesh):
    blocks, pops = mesh.shape["genome"], mesh.shape["ancestry"]
    members = blocks * pops

    def body(zscores, ld_diag, ld_next, prior_precision, chrom_cut, band_width):
        _, traits, length = zscores.shape
        bf16, f32 = jnp.bfloat16, jnp.float32
        dma = pltpu.SemaphoreType.DMA
        others = max(pops - 1, 1)
        return pl.pallas_call(
            functools.partial(kernel, blocks, pops),
            out_shape=jax.ShapeDtypeStruct(zscores.shape, f32),
            in_specs=[pl.BlockSpec(memory_space=pltpu.SMEM)] * 3
            + [pl.BlockSpec(memory_space=pl.ANY)] * 3,
            out_specs=pl.BlockSpec(memory_space=pltpu.VMEM),
            scratch_shapes=[
                pltpu.VMEM((traits, length), f32),
                pltpu.VMEM((length, length), bf16),
                pltpu.VMEM((length, length), bf16),
                pltpu.VMEM((1, length), f32),
                pltpu.VMEM((3, traits, length), f32),
                pltpu.VMEM((3, traits, length), bf16),
                pltpu.VMEM((3, traits, length), f32),
                pltpu.VMEM((3, traits, length), bf16),
                pltpu.VMEM((3, others, traits, length), bf16),
                pltpu.VMEM((2, traits, length), bf16),
                pltpu.VMEM((2, traits, length), bf16),
                pltpu.VMEM((members, 8, LANES), f32),
                pltpu.VMEM((members, 1, LANES), f32),
                dma((3,)), dma((3,)), dma((3,)),
                dma((3, others)), dma((3, others)),
                dma((2,)), dma((2,)),
                dma((members,)), dma((members,)), dma((members,)), dma((members,)),
            ],
            compiler_params=pltpu.CompilerParams(
                collective_id=0, has_side_effects=True, vmem_limit_bytes=32 << 20
            ),
        )(prior_precision, chrom_cut, band_width, zscores, ld_diag, ld_next)

    return jax.shard_map(
        body,
        mesh=mesh,
        in_specs=(
            P("ancestry", "trait", ("groups", "genome")),
            P("ancestry", ("groups", "genome"), None),
            P("ancestry", ("groups", "genome"), None),
            P(),
            P("groups"),
            P("groups"),
        ),
        out_specs=P("ancestry", "trait", ("groups", "genome")),
        check_vma=False,
    )
```

```python
import functools

import jax
import jax.numpy as jnp
from jax import lax
from jax.experimental import pallas as pl
from jax.experimental.pallas import tpu as pltpu
from jax.sharding import PartitionSpec as P

MESH = pl.DeviceIdType.MESH
COLS = 256
ROWS = 32
LANES = 128
UNROLL_PEERS = 16


def for_each(start, stop, step_fn):
    if stop - start <= UNROLL_PEERS:
        for index in range(start, stop):
            step_fn(index)
    else:
        lax.fori_loop(start, stop, lambda index, carry: (step_fn(index), carry)[1], 0)


def kernel(
    blocks, pops,
    prior_hbm, cuts_hbm, widths_hbm, z_hbm, diag_hbm, next_hbm,
    out_ref,
    prior, cuts, widths, zv, blocks_on, dv, nv, scale, p, pb, image, up, anc, carry_out, carry_in, sums, tail,
    load_sem, up_send, up_recv, anc_send, anc_recv, carry_send, carry_recv,
    sums_send, sums_recv, tail_send, tail_recv,
):
    traits, length = zv.shape
    members = blocks * pops
    pos = lax.axis_index("genome")
    pop = lax.axis_index("ancestry")
    before = jnp.maximum(pos - 1, 0)
    after = jnp.minimum(pos + 1, blocks - 1)

    chunks = length // COLS
    small = [(prior_hbm, prior), (cuts_hbm, cuts), (widths_hbm, widths), (z_hbm.at[0], zv)]
    for b in range(length // LANES):
        at = pl.ds(b * LANES, LANES)
        small.append((diag_hbm.at[0, at, at], blocks_on.at[b]))
    large = []
    for src, dst in ((next_hbm, nv), (diag_hbm, dv)):
        for b in range(chunks):
            at = pl.ds(b * COLS, COLS)
            large.append((src.at[0, at], dst.at[at]))
    loads = [
        pltpu.make_async_copy(src, dst, load_sem.at[i])
        for i, (src, dst) in enumerate(small + large)
    ]
    for load in loads:
        load.start()
    next_loads = loads[len(small) : len(small) + chunks]
    diag_loads = loads[len(small) + chunks :]

    def peer(offset):
        return {
            "genome": lax.rem(pos + offset // pops, blocks),
            "ancestry": lax.rem(pop + offset % pops, pops),
        }

    barrier = pltpu.get_barrier_semaphore()
    for_each(
        1, members,
        lambda k: pl.semaphore_signal(barrier, inc=1, device_id=peer(k), device_id_type=MESH),
    )

    def up_copy(k, j):
        return pltpu.make_async_remote_copy(
            pb.at[k, j], up.at[k, j], up_send.at[k, j], up_recv.at[k, j],
            device_id={"genome": before}, device_id_type=MESH,
        )

    def carry_copy(k, j):
        return pltpu.make_async_remote_copy(
            carry_out.at[k, j], carry_in.at[k, j], carry_send.at[k, j], carry_recv.at[k, j],
            device_id={"genome": after}, device_id_type=MESH,
        )

    def anc_copy(k, j, shift):
        return pltpu.make_async_remote_copy(
            pb.at[k, j], anc.at[k, j, shift - 1],
            anc_send.at[k, j, shift - 1], anc_recv.at[k, j, shift - 1],
            device_id={"ancestry": lax.rem(pop + shift, pops)}, device_id_type=MESH,
        )

    def sums_copy(k):
        return pltpu.make_async_remote_copy(
            sums.at[0], sums.at[k], sums_send.at[k], sums_recv.at[k],
            device_id=peer(k), device_id_type=MESH,
        )

    def tail_copy(k):
        return pltpu.make_async_remote_copy(
            tail.at[0], tail.at[k], tail_send.at[k], tail_recv.at[k],
            device_id=peer(k), device_id_type=MESH,
        )

    has_before = pos > 0
    has_after = pos < blocks - 1

    @pl.when(pos == blocks - 1)
    def _():
        up[...] = jnp.zeros_like(up)

    @pl.when(pos == 0)
    def _():
        carry_in[...] = jnp.zeros_like(carry_in)

    def span(j):
        return pl.ds(j * COLS, COLS)

    def send_direction(k, j):
        @pl.when(has_before)
        def _():
            up_copy(k, j).start()

        for shift in range(1, pops):
            anc_copy(k, j, shift).start()

    def whole(ref, k):
        return jnp.concatenate([ref[k, j] for j in range(chunks)], axis=1)

    for load in loads[: len(small)]:
        load.wait()
    cut_here, cut_after = cuts[pos], cuts[after]
    width_here = widths[pos]
    width_both = jnp.minimum(width_here, widths[after])
    cut_here = jnp.minimum(cut_here, length)
    cut_after = jnp.where(has_after, jnp.minimum(cut_after, length), 0)

    self_weight = prior[pop, pop]
    eye = lax.broadcasted_iota(jnp.int32, (LANES, LANES), 0) == lax.broadcasted_iota(
        jnp.int32, (LANES, LANES), 1
    )
    for b in range(length // LANES):
        at = pl.ds(b * LANES, LANES)
        tile = jnp.where(eye, blocks_on[b].astype(jnp.float32), 0.0)
        scale[:, at] = 1.0 / (jnp.sum(tile, axis=0, keepdims=True) + self_weight)
    p[0] = scale[...] * zv[...]
    for j in range(chunks):
        pb[0, j] = p[0, :, span(j)].astype(jnp.bfloat16)

    pl.semaphore_wait(barrier, members - 1)
    for j in range(chunks):
        send_direction(0, j)

    col_ids = lax.broadcasted_iota(jnp.int32, (ROWS, length), 1)
    row_base = lax.broadcasted_iota(jnp.int32, (ROWS, 1), 0)

    def mask_next(i, carry):
        at = pl.ds(pl.multiple_of(i * ROWS, ROWS), ROWS)
        rows = row_base + i * ROWS
        opened = (rows < cut_here) & (cut_here < length)
        high = jnp.minimum(width_both - length + rows, cut_after)
        high = jnp.where(opened, 0, high)
        tile = nv[at, :].astype(jnp.float32)
        nv[at, :] = jnp.where(col_ids < high, tile, 0.0).astype(jnp.bfloat16)
        return carry

    for b in range(chunks):
        next_loads[b].wait()
        lax.fori_loop(b * COLS // ROWS, (b + 1) * COLS // ROWS, mask_next, 0)

    def send_carry(k):
        direction = whole(pb, k)
        for j in range(chunks):
            carry_out[k, j] = jnp.dot(
                direction, nv[:, span(j)], preferred_element_type=jnp.float32
            ).astype(jnp.bfloat16)

            @pl.when(has_after)
            def _():
                carry_copy(k, j).start()

    send_carry(0)

    def mask_diag(i, carry):
        at = pl.ds(pl.multiple_of(i * ROWS, ROWS), ROWS)
        rows = row_base + i * ROWS
        left = rows < cut_here
        low = jnp.maximum(rows - width_here + 1, jnp.where(left, 0, cut_here))
        high = jnp.minimum(rows + width_here, jnp.where(left, cut_here, length))
        tile = dv[at, :].astype(jnp.float32)
        keep = (col_ids >= low) & (col_ids < high)
        dv[at, :] = jnp.where(keep, tile, 0.0).astype(jnp.bfloat16)
        return carry

    for load in diag_loads:
        load.wait()
    lax.fori_loop(0, length // ROWS, mask_diag, 0)

    def dot_diag(k):
        direction = whole(pb, k)
        for j in range(chunks):
            image[k, :, span(j)] = self_weight * pb[k, j].astype(jnp.float32) + jnp.dot(
                direction, dv[:, span(j)], preferred_element_type=jnp.float32
            )

    def dot_up(k):
        total = None
        for j in range(chunks):
            @pl.when(has_after)
            def _():
                up_copy(k, j).wait_recv()

            part = lax.dot_general(
                up[k, j], nv[:, span(j)], (((1,), (1,)), ((), ())),
                preferred_element_type=jnp.float32,
            )
            total = part if total is None else total + part
        return total

    def coupled(k, j):
        total = 0.0
        for shift in range(1, pops):
            anc_copy(k, j, shift).wait_recv()
            other = lax.rem(pop + pops - shift, pops)
            total = total + prior[pop, other] * anc[k, j, shift - 1].astype(jnp.float32)
        return total

    def inner(left, right):
        return jnp.sum(left * right, axis=1, keepdims=True)

    for k in range(2):
        if k > 0:
            send_carry(k)
        dot_diag(k)
        image[k] = image[k] + dot_up(k)
        for j in range(chunks):
            both = image[k, :, span(j)] + coupled(k, j)

            @pl.when(has_before)
            def _():
                carry_copy(k, j).wait_recv()

            both = both + carry_in[k, j].astype(jnp.float32)
            image[k, :, span(j)] = both
            following = scale[:, span(j)] * both - p[k, :, span(j)]
            p[k + 1, :, span(j)] = following
            pb[k + 1, j] = following.astype(jnp.bfloat16)
            send_direction(k + 1, j)

    lane_ids = lax.broadcasted_iota(jnp.int32, (traits, LANES), 1)

    def as_rows(columns):
        packed = jnp.zeros((traits, LANES), jnp.float32)
        for j, column in enumerate(columns):
            packed = jnp.where(lane_ids == j, column, packed)
        packed = jnp.concatenate(
            [packed, jnp.zeros((LANES - traits, LANES), jnp.float32)], axis=0
        )
        return jnp.transpose(packed)[:8]

    sums[0] = as_rows([
        inner(p[0], zv[...]), inner(p[1], zv[...]), inner(p[2], zv[...]),
        inner(p[0], image[0]), inner(p[0], image[1]), inner(p[1], image[1]),
        inner(p[2], image[0]), inner(p[2], image[1]),
    ])
    for_each(1, members, lambda k: sums_copy(k).start())

    dot_diag(2)
    other_part = jnp.concatenate([coupled(2, j) for j in range(chunks)], axis=1)
    last = inner(p[2], image[2] + 2.0 * dot_up(2) + other_part)
    tail[0] = as_rows([last])[:1]
    for_each(1, members, lambda k: tail_copy(k).start())

    for_each(1, members, lambda k: sums_copy(k).wait_recv())
    total = jnp.sum(sums[...], axis=0)
    b0, b1, b2, g00, g01, g11, g02, g12 = (total[j : j + 1] for j in range(8))
    l10 = g01 / g00
    d1 = g11 - l10 * g01
    l20 = g02 / g00
    cross = g12 - l20 * g01
    l21 = cross / d1
    y1 = b1 - l10 * b0
    y2 = b2 - l20 * b0 - l21 * y1
    known = l20 * g02 + l21 * cross
    z0 = b0 / g00
    z1 = y1 / d1

    for_each(1, members, lambda k: tail_copy(k).wait_recv())
    g22 = jnp.sum(tail[...], axis=0)
    c2 = y2 / (g22 - known)
    c1 = z1 - l21 * c2
    c0 = z0 - l10 * c1 - l20 * c2
    stacked = jnp.concatenate(
        [c0, c1, c2, jnp.zeros((LANES - 3, LANES), jnp.float32)], axis=0
    )
    stacked = jnp.transpose(stacked)[:traits]
    out_ref[0] = (
        stacked[:, 0:1] * p[0] + stacked[:, 1:2] * p[1] + stacked[:, 2:3] * p[2]
    )

    for k in range(3):
        for j in range(chunks):
            @pl.when(has_before)
            def _():
                up_copy(k, j).wait_send()

            for shift in range(1, pops):
                anc_copy(k, j, shift).wait_send()
    for k in range(2):
        for j in range(chunks):
            @pl.when(has_after)
            def _():
                carry_copy(k, j).wait_send()
    for_each(1, members, lambda k: sums_copy(k).wait_send())
    for_each(1, members, lambda k: tail_copy(k).wait_send())


def solution(mesh):
    blocks, pops = mesh.shape["genome"], mesh.shape["ancestry"]
    members = blocks * pops

    def body(zscores, ld_diag, ld_next, prior_precision, chrom_cut, band_width):
        _, traits, length = zscores.shape
        bf16, f32 = jnp.bfloat16, jnp.float32
        dma = pltpu.SemaphoreType.DMA
        others = max(pops - 1, 1)
        chunks = length // COLS
        return pl.pallas_call(
            functools.partial(kernel, blocks, pops),
            out_shape=jax.ShapeDtypeStruct(zscores.shape, f32),
            in_specs=[pl.BlockSpec(memory_space=pltpu.HBM)] * 6,
            out_specs=pl.BlockSpec(memory_space=pltpu.VMEM),
            scratch_shapes=[
                pltpu.SMEM(prior_precision.shape, f32),
                pltpu.SMEM(chrom_cut.shape, jnp.int32),
                pltpu.SMEM(band_width.shape, jnp.int32),
                pltpu.VMEM((traits, length), f32),
                pltpu.VMEM((length // LANES, LANES, LANES), bf16),
                pltpu.VMEM((length, length), bf16),
                pltpu.VMEM((length, length), bf16),
                pltpu.VMEM((1, length), f32),
                pltpu.VMEM((3, traits, length), f32),
                pltpu.VMEM((3, chunks, traits, COLS), bf16),
                pltpu.VMEM((3, traits, length), f32),
                pltpu.VMEM((3, chunks, traits, COLS), bf16),
                pltpu.VMEM((3, chunks, others, traits, COLS), bf16),
                pltpu.VMEM((2, chunks, traits, COLS), bf16),
                pltpu.VMEM((2, chunks, traits, COLS), bf16),
                pltpu.VMEM((members, 8, LANES), f32),
                pltpu.VMEM((members, 1, LANES), f32),
                dma((4 + length // LANES + 2 * chunks,)),
                dma((3, chunks)), dma((3, chunks)),
                dma((3, chunks, others)), dma((3, chunks, others)),
                dma((2, chunks)), dma((2, chunks)),
                dma((members,)), dma((members,)), dma((members,)), dma((members,)),
            ],
            compiler_params=pltpu.CompilerParams(
                collective_id=0, has_side_effects=True, vmem_limit_bytes=64 << 20
            ),
        )(prior_precision, chrom_cut, band_width, zscores, ld_diag, ld_next)

    return jax.shard_map(
        body,
        mesh=mesh,
        in_specs=(
            P("ancestry", "trait", ("groups", "genome")),
            P("ancestry", ("groups", "genome"), None),
            P("ancestry", ("groups", "genome"), None),
            P(),
            P("groups"),
            P("groups"),
        ),
        out_specs=P("ancestry", "trait", ("groups", "genome")),
        check_vma=False,
    )
```

```python
import functools

import jax
import jax.numpy as jnp
from jax import lax
from jax.experimental import pallas as pl
from jax.experimental.pallas import tpu as pltpu
from jax.sharding import PartitionSpec as P

MESH = pl.DeviceIdType.MESH
COLS = 512
ROWS = 64
LANES = 128
UNROLL_PEERS = 16


def for_each(start, stop, step_fn):
    if stop - start <= UNROLL_PEERS:
        for index in range(start, stop):
            step_fn(index)
    else:
        lax.fori_loop(start, stop, lambda index, carry: (step_fn(index), carry)[1], 0)


def kernel(
    blocks, pops,
    prior_hbm, cuts_hbm, widths_hbm, z_hbm, diag_hbm, next_hbm,
    out_ref,
    prior, cuts, widths, zv, dv, nv, tv, scale, p, pb, image, up, anc, carry_out, carry_in, sums, tail,
    load_sem, up_send, up_recv, anc_send, anc_recv, carry_send, carry_recv,
    sums_send, sums_recv, tail_send, tail_recv,
):
    traits, length = zv.shape
    members = blocks * pops
    pos = lax.axis_index("genome")
    pop = lax.axis_index("ancestry")
    before = jnp.maximum(pos - 1, 0)
    after = jnp.minimum(pos + 1, blocks - 1)

    chunks = length // COLS
    small = [(prior_hbm, prior), (cuts_hbm, cuts), (widths_hbm, widths), (z_hbm.at[0], zv)]
    large = []
    for src, dst in ((diag_hbm, dv), (next_hbm, nv)):
        for b in range(chunks):
            at = pl.ds(b * COLS, COLS)
            large.append((src.at[0, at], dst.at[at]))
    loads = [
        pltpu.make_async_copy(src, dst, load_sem.at[i])
        for i, (src, dst) in enumerate(small + large)
    ]
    for load in loads:
        load.start()
    next_loads = loads[len(small) + chunks :]

    me = pos * pops + pop
    late = pos >= blocks // 2

    def peer(offset):
        jump = blocks - 1 - offset // pops
        jump = jnp.where(late, blocks - jump, jump)
        return {
            "genome": lax.rem(pos + jump, blocks),
            "ancestry": lax.rem(pop + pops - 1 - offset % pops, pops),
        }

    def sent_by(offset):
        jump = offset // pops
        there = lax.rem(pos + jump, blocks) * pops + lax.rem(pop + offset % pops, pops)
        return there

    barrier = pltpu.get_barrier_semaphore()
    for_each(
        0, members - 1,
        lambda k: pl.semaphore_signal(barrier, inc=1, device_id=peer(k), device_id_type=MESH),
    )

    def up_copy(k, j):
        return pltpu.make_async_remote_copy(
            pb.at[k, j], up.at[k, j], up_send.at[k, j], up_recv.at[k, j],
            device_id={"genome": before}, device_id_type=MESH,
        )

    def carry_copy(k, j):
        return pltpu.make_async_remote_copy(
            carry_out.at[k, j], carry_in.at[k, j], carry_send.at[k, j], carry_recv.at[k, j],
            device_id={"genome": after}, device_id_type=MESH,
        )

    def anc_copy(k, shift):
        return pltpu.make_async_remote_copy(
            pb.at[k], anc.at[k, shift - 1], anc_send.at[k, shift - 1], anc_recv.at[k, shift - 1],
            device_id={"ancestry": lax.rem(pop + shift, pops)}, device_id_type=MESH,
        )

    def sums_copy(k):
        return pltpu.make_async_remote_copy(
            sums.at[me], sums.at[me], sums_send.at[k], sums_recv.at[me],
            device_id=peer(k), device_id_type=MESH,
        )

    def tail_copy(k):
        return pltpu.make_async_remote_copy(
            tail.at[me], tail.at[me], tail_send.at[k], tail_recv.at[me],
            device_id=peer(k), device_id_type=MESH,
        )

    def arrival(ref, send_sem, recv_sem, k):
        slot = sent_by(k)
        return pltpu.make_async_remote_copy(
            ref.at[slot], ref.at[slot], send_sem.at[0], recv_sem.at[slot],
            device_id=peer(0), device_id_type=MESH,
        )

    has_before = pos > 0
    has_after = pos < blocks - 1

    @pl.when(pos == blocks - 1)
    def _():
        up[...] = jnp.zeros_like(up)

    @pl.when(pos == 0)
    def _():
        carry_in[...] = jnp.zeros_like(carry_in)

    def span(j):
        return pl.ds(j * COLS, COLS)

    def send_direction(k, j):
        @pl.when(has_before)
        def _():
            up_copy(k, j).start()

        if j == chunks - 1:
            for shift in range(1, pops):
                anc_copy(k, shift).start()

    def whole(ref, k):
        return jnp.concatenate([ref[k, j] for j in range(chunks)], axis=1)

    for load in loads[: len(small) + chunks]:
        load.wait()
    cut_here, cut_after = cuts[pos], cuts[after]
    width_here = widths[pos]
    width_both = jnp.minimum(width_here, widths[after])
    cut_here = jnp.minimum(cut_here, length)
    cut_after = jnp.where(has_after, jnp.minimum(cut_after, length), 0)

    self_weight = prior[pop, pop]
    eye = lax.broadcasted_iota(jnp.int32, (LANES, LANES), 0) == lax.broadcasted_iota(
        jnp.int32, (LANES, LANES), 1
    )
    for b in range(length // LANES):
        at = pl.ds(b * LANES, LANES)
        tile = jnp.where(eye, dv[at, at].astype(jnp.float32), 0.0)
        scale[:, at] = 1.0 / (jnp.sum(tile, axis=0, keepdims=True) + self_weight)
    p[0] = scale[...] * zv[...]
    for j in range(chunks):
        pb[0, j] = p[0, :, span(j)].astype(jnp.bfloat16)

    pl.semaphore_wait(barrier, members - 1)
    for j in range(chunks):
        send_direction(0, j)

    col_ids = lax.broadcasted_iota(jnp.int32, (ROWS, length), 1)
    row_base = lax.broadcasted_iota(jnp.int32, (ROWS, 1), 0)

    def mask_next(i, carry):
        at = pl.ds(pl.multiple_of(i * ROWS, ROWS), ROWS)
        rows = row_base + i * ROWS
        opened = (rows < cut_here) & (cut_here < length)
        high = jnp.minimum(width_both - length + rows, cut_after)
        high = jnp.where(opened, 0, high)
        tile = nv[at, :].astype(jnp.float32)
        nv[at, :] = jnp.where(col_ids < high, tile, 0.0).astype(jnp.bfloat16)
        return carry

    for b in range(chunks):
        next_loads[b].wait()
        lax.fori_loop(b * COLS // ROWS, (b + 1) * COLS // ROWS, mask_next, 0)

    def send_carry(k):
        direction = whole(pb, k)
        for j in range(chunks):
            carry_out[k, j] = jnp.dot(
                direction, nv[:, span(j)], preferred_element_type=jnp.float32
            ).astype(jnp.bfloat16)

            @pl.when(has_after)
            def _():
                carry_copy(k, j).start()

    send_carry(0)

    def mask_diag(i, carry):
        at = pl.ds(pl.multiple_of(i * ROWS, ROWS), ROWS)
        rows = row_base + i * ROWS
        left = rows < cut_here
        low = jnp.maximum(rows - width_here + 1, jnp.where(left, 0, cut_here))
        high = jnp.minimum(rows + width_here, jnp.where(left, cut_here, length))
        tile = dv[at, :].astype(jnp.float32)
        keep = (col_ids >= low) & (col_ids < high)
        dv[at, :] = jnp.where(keep, tile, 0.0).astype(jnp.bfloat16)
        return carry

    lax.fori_loop(0, length // ROWS, mask_diag, 0)

    def dot_diag(k):
        direction = whole(pb, k)
        for j in range(chunks):
            image[k, :, span(j)] = self_weight * pb[k, j].astype(jnp.float32) + jnp.dot(
                direction, dv[:, span(j)], preferred_element_type=jnp.float32
            )

    def dot_up(k):
        total = None
        for j in range(chunks):
            @pl.when(has_after)
            def _():
                up_copy(k, j).wait_recv()

            if k == 0:
                part = lax.dot_general(
                    up[k, j], nv[:, span(j)], (((1,), (1,)), ((), ())),
                    preferred_element_type=jnp.float32,
                )
            else:
                part = jnp.dot(up[k, j], tv[span(j)], preferred_element_type=jnp.float32)
            total = part if total is None else total + part
        return total

    def coupled(k, j):
        total = 0.0
        for shift in range(1, pops):
            if j == 0:
                anc_copy(k, shift).wait_recv()
            other = lax.rem(pop + pops - shift, pops)
            total = total + prior[pop, other] * anc[k, shift - 1, j].astype(jnp.float32)
        return total

    def turn_next():
        for i in range(length // LANES):
            at = pl.ds(i * LANES, LANES)
            tv[at] = jnp.transpose(nv[:, at])

    def inner(left, right):
        return jnp.sum(left * right, axis=1, keepdims=True)

    for k in range(2):
        if k > 0:
            send_carry(k)
        dot_diag(k)
        if k == 1:
            turn_next()
        image[k] = image[k] + dot_up(k)
        for j in range(chunks):
            both = image[k, :, span(j)] + coupled(k, j)

            @pl.when(has_before)
            def _():
                carry_copy(k, j).wait_recv()

            both = both + carry_in[k, j].astype(jnp.float32)
            image[k, :, span(j)] = both
            following = scale[:, span(j)] * both - p[k, :, span(j)]
            p[k + 1, :, span(j)] = following
            pb[k + 1, j] = following.astype(jnp.bfloat16)
            send_direction(k + 1, j)

    lane_ids = lax.broadcasted_iota(jnp.int32, (traits, LANES), 1)

    def as_rows(columns):
        packed = jnp.zeros((traits, LANES), jnp.float32)
        for j, column in enumerate(columns):
            packed = jnp.where(lane_ids == j, column, packed)
        packed = jnp.concatenate(
            [packed, jnp.zeros((LANES - traits, LANES), jnp.float32)], axis=0
        )
        return jnp.transpose(packed)[:8]

    sums[me] = as_rows([
        inner(p[0], zv[...]), inner(p[1], zv[...]), inner(p[2], zv[...]),
        inner(p[0], image[0]), inner(p[0], image[1]), inner(p[1], image[1]),
        inner(p[2], image[0]), inner(p[2], image[1]),
    ])
    for_each(0, members - 1, lambda k: sums_copy(k).start())

    dot_diag(2)
    other_part = jnp.concatenate([coupled(2, j) for j in range(chunks)], axis=1)
    last = inner(p[2], image[2] + 2.0 * dot_up(2) + other_part)
    tail[me] = as_rows([last])[:1]
    for_each(0, members - 1, lambda k: tail_copy(k).start())

    for_each(1, members, lambda k: arrival(sums, sums_send, sums_recv, k).wait_recv())
    total = jnp.sum(sums[...], axis=0)
    b0, b1, b2, g00, g01, g11, g02, g12 = (total[j : j + 1] for j in range(8))
    l10 = g01 / g00
    d1 = g11 - l10 * g01
    l20 = g02 / g00
    cross = g12 - l20 * g01
    l21 = cross / d1
    y1 = b1 - l10 * b0
    y2 = b2 - l20 * b0 - l21 * y1
    known = l20 * g02 + l21 * cross
    z0 = b0 / g00
    z1 = y1 / d1

    for_each(1, members, lambda k: arrival(tail, tail_send, tail_recv, k).wait_recv())
    g22 = jnp.sum(tail[...], axis=0)
    c2 = y2 / (g22 - known)
    c1 = z1 - l21 * c2
    c0 = z0 - l10 * c1 - l20 * c2
    stacked = jnp.concatenate(
        [c0, c1, c2, jnp.zeros((LANES - 3, LANES), jnp.float32)], axis=0
    )
    stacked = jnp.transpose(stacked)[:traits]
    out_ref[0] = (
        stacked[:, 0:1] * p[0] + stacked[:, 1:2] * p[1] + stacked[:, 2:3] * p[2]
    )

    for k in range(3):
        for j in range(chunks):
            @pl.when(has_before)
            def _():
                up_copy(k, j).wait_send()

        for shift in range(1, pops):
            anc_copy(k, shift).wait_send()
    for k in range(2):
        for j in range(chunks):
            @pl.when(has_after)
            def _():
                carry_copy(k, j).wait_send()
    for_each(0, members - 1, lambda k: sums_copy(k).wait_send())
    for_each(0, members - 1, lambda k: tail_copy(k).wait_send())


def solution(mesh):
    blocks, pops = mesh.shape["genome"], mesh.shape["ancestry"]
    members = blocks * pops

    def body(zscores, ld_diag, ld_next, prior_precision, chrom_cut, band_width):
        _, traits, length = zscores.shape
        bf16, f32 = jnp.bfloat16, jnp.float32
        dma = pltpu.SemaphoreType.DMA
        others = max(pops - 1, 1)
        chunks = length // COLS
        return pl.pallas_call(
            functools.partial(kernel, blocks, pops),
            out_shape=jax.ShapeDtypeStruct(zscores.shape, f32),
            in_specs=[pl.BlockSpec(memory_space=pltpu.HBM)] * 6,
            out_specs=pl.BlockSpec(memory_space=pltpu.VMEM),
            scratch_shapes=[
                pltpu.SMEM(prior_precision.shape, f32),
                pltpu.SMEM(chrom_cut.shape, jnp.int32),
                pltpu.SMEM(band_width.shape, jnp.int32),
                pltpu.VMEM((traits, length), f32),
                pltpu.VMEM((length, length), bf16),
                pltpu.VMEM((length, length), bf16),
                pltpu.VMEM((length, length), bf16),
                pltpu.VMEM((1, length), f32),
                pltpu.VMEM((3, traits, length), f32),
                pltpu.VMEM((3, chunks, traits, COLS), bf16),
                pltpu.VMEM((3, traits, length), f32),
                pltpu.VMEM((3, chunks, traits, COLS), bf16),
                pltpu.VMEM((3, others, chunks, traits, COLS), bf16),
                pltpu.VMEM((2, chunks, traits, COLS), bf16),
                pltpu.VMEM((2, chunks, traits, COLS), bf16),
                pltpu.VMEM((members, 8, LANES), f32),
                pltpu.VMEM((members, 1, LANES), f32),
                dma((4 + 2 * chunks,)),
                dma((3, chunks)), dma((3, chunks)),
                dma((3, others)), dma((3, others)),
                dma((2, chunks)), dma((2, chunks)),
                dma((members,)), dma((members,)), dma((members,)), dma((members,)),
            ],
            compiler_params=pltpu.CompilerParams(
                collective_id=0, has_side_effects=True, vmem_limit_bytes=64 << 20
            ),
        )(prior_precision, chrom_cut, band_width, zscores, ld_diag, ld_next)

    return jax.shard_map(
        body,
        mesh=mesh,
        in_specs=(
            P("ancestry", "trait", ("groups", "genome")),
            P("ancestry", ("groups", "genome"), None),
            P("ancestry", ("groups", "genome"), None),
            P(),
            P("groups"),
            P("groups"),
        ),
        out_specs=P("ancestry", "trait", ("groups", "genome")),
        check_vma=False,
    )
```

```python
import functools

import jax
import jax.numpy as jnp
from jax import lax
from jax.experimental import pallas as pl
from jax.experimental.pallas import tpu as pltpu
from jax.sharding import PartitionSpec as P

MESH = pl.DeviceIdType.MESH
COLS = 512
ROWS = 64
LANES = 128
UNROLL_PEERS = 16


def for_each(start, stop, step_fn):
    if stop - start <= UNROLL_PEERS:
        for index in range(start, stop):
            step_fn(index)
    else:
        lax.fori_loop(start, stop, lambda index, carry: (step_fn(index), carry)[1], 0)


def kernel(
    blocks, pops,
    prior_hbm, cuts_hbm, widths_hbm, z_hbm, diag_hbm, next_hbm,
    out_ref,
    prior, cuts, widths, zv, dv, nv, tv, scale, p, pb, image, up, anc, carry_out, carry_in, sums, tail,
    load_sem, up_send, up_recv, anc_send, anc_recv, carry_send, carry_recv,
    sums_send, sums_recv, tail_send, tail_recv,
):
    traits, length = zv.shape
    members = blocks * pops
    pos = lax.axis_index("genome")
    pop = lax.axis_index("ancestry")
    before = jnp.maximum(pos - 1, 0)
    after = jnp.minimum(pos + 1, blocks - 1)

    chunks = length // COLS
    small = [(prior_hbm, prior), (cuts_hbm, cuts), (widths_hbm, widths), (z_hbm.at[0], zv)]
    large = []
    for src, dst in ((diag_hbm, dv), (next_hbm, nv)):
        for b in range(chunks):
            at = pl.ds(b * COLS, COLS)
            large.append((src.at[0, at], dst.at[at]))
    loads = [
        pltpu.make_async_copy(src, dst, load_sem.at[i])
        for i, (src, dst) in enumerate(small + large)
    ]
    for load in loads:
        load.start()
    next_loads = loads[len(small) + chunks :]

    me = pos * pops + pop
    late = pos >= blocks // 2

    def peer(offset):
        jump = blocks - 1 - offset // pops
        jump = jnp.where(late, blocks - jump, jump)
        return {
            "genome": lax.rem(pos + jump, blocks),
            "ancestry": lax.rem(pop + pops - 1 - offset % pops, pops),
        }

    def sent_by(offset):
        jump = offset // pops
        there = lax.rem(pos + jump, blocks) * pops + lax.rem(pop + offset % pops, pops)
        return there

    barrier = pltpu.get_barrier_semaphore()
    for_each(
        0, members - 1,
        lambda k: pl.semaphore_signal(barrier, inc=1, device_id=peer(k), device_id_type=MESH),
    )

    def up_copy(k, j):
        return pltpu.make_async_remote_copy(
            pb.at[k, j], up.at[k, j], up_send.at[k, j], up_recv.at[k, j],
            device_id={"genome": before}, device_id_type=MESH,
        )

    def carry_copy(k, j):
        return pltpu.make_async_remote_copy(
            carry_out.at[k, j], carry_in.at[k, j], carry_send.at[k, j], carry_recv.at[k, j],
            device_id={"genome": after}, device_id_type=MESH,
        )

    def anc_copy(k, shift):
        return pltpu.make_async_remote_copy(
            pb.at[k], anc.at[k, shift - 1], anc_send.at[k, shift - 1], anc_recv.at[k, shift - 1],
            device_id={"ancestry": lax.rem(pop + shift, pops)}, device_id_type=MESH,
        )

    def sums_copy(k):
        return pltpu.make_async_remote_copy(
            sums.at[me], sums.at[me], sums_send.at[k], sums_recv.at[me],
            device_id=peer(k), device_id_type=MESH,
        )

    def tail_copy(k):
        return pltpu.make_async_remote_copy(
            tail.at[me], tail.at[me], tail_send.at[k], tail_recv.at[me],
            device_id=peer(k), device_id_type=MESH,
        )

    def arrival(ref, send_sem, recv_sem, k):
        slot = sent_by(k)
        return pltpu.make_async_remote_copy(
            ref.at[slot], ref.at[slot], send_sem.at[0], recv_sem.at[slot],
            device_id=peer(0), device_id_type=MESH,
        )

    has_before = pos > 0
    has_after = pos < blocks - 1

    @pl.when(pos == blocks - 1)
    def _():
        up[...] = jnp.zeros_like(up)

    @pl.when(pos == 0)
    def _():
        carry_in[...] = jnp.zeros_like(carry_in)

    def span(j):
        return pl.ds(j * COLS, COLS)

    def send_direction(k, j):
        @pl.when(has_before)
        def _():
            up_copy(k, j).start()

        if j == chunks - 1:
            for shift in range(1, pops):
                anc_copy(k, shift).start()

    def whole(ref, k):
        return jnp.concatenate([ref[k, j] for j in range(chunks)], axis=1)

    for load in loads[: len(small) + chunks]:
        load.wait()
    cut_here, cut_after = cuts[pos], cuts[after]
    width_here = widths[pos]
    width_both = jnp.minimum(width_here, widths[after])
    cut_here = jnp.minimum(cut_here, length)
    cut_after = jnp.where(has_after, jnp.minimum(cut_after, length), 0)

    self_weight = prior[pop, pop]
    eye = lax.broadcasted_iota(jnp.int32, (LANES, LANES), 0) == lax.broadcasted_iota(
        jnp.int32, (LANES, LANES), 1
    )
    for b in range(length // LANES):
        at = pl.ds(b * LANES, LANES)
        tile = jnp.where(eye, dv[at, at].astype(jnp.float32), 0.0)
        scale[:, at] = 1.0 / (jnp.sum(tile, axis=0, keepdims=True) + self_weight)
    p[0] = scale[...] * zv[...]
    for j in range(chunks):
        pb[0, j] = p[0, :, span(j)].astype(jnp.bfloat16)

    pl.semaphore_wait(barrier, members - 1)
    for j in range(chunks):
        send_direction(0, j)

    col_ids = lax.broadcasted_iota(jnp.int32, (ROWS, length), 1)
    row_base = lax.broadcasted_iota(jnp.int32, (ROWS, 1), 0)

    def mask_next(i, carry):
        at = pl.ds(pl.multiple_of(i * ROWS, ROWS), ROWS)
        rows = row_base + i * ROWS
        opened = (rows < cut_here) & (cut_here < length)
        high = jnp.minimum(width_both - length + rows, cut_after)
        high = jnp.where(opened, 0, high)
        tile = nv[at, :].astype(jnp.float32)
        nv[at, :] = jnp.where(col_ids < high, tile, 0.0).astype(jnp.bfloat16)
        return carry

    for b in range(chunks):
        next_loads[b].wait()
        lax.fori_loop(b * COLS // ROWS, (b + 1) * COLS // ROWS, mask_next, 0)

    def send_carry(k):
        direction = whole(pb, k)
        for j in range(chunks):
            carry_out[k, j] = jnp.dot(
                direction, nv[:, span(j)], preferred_element_type=jnp.float32
            ).astype(jnp.bfloat16)

            @pl.when(has_after)
            def _():
                carry_copy(k, j).start()

    send_carry(0)

    def mask_diag(i, carry):
        at = pl.ds(pl.multiple_of(i * ROWS, ROWS), ROWS)
        rows = row_base + i * ROWS
        left = rows < cut_here
        low = jnp.maximum(rows - width_here + 1, jnp.where(left, 0, cut_here))
        high = jnp.minimum(rows + width_here, jnp.where(left, cut_here, length))
        tile = dv[at, :].astype(jnp.float32)
        keep = (col_ids >= low) & (col_ids < high)
        dv[at, :] = jnp.where(keep, tile, 0.0).astype(jnp.bfloat16)
        return carry

    lax.fori_loop(0, length // ROWS, mask_diag, 0)

    def dot_diag(k):
        direction = whole(pb, k)
        for j in range(chunks):
            image[k, :, span(j)] = self_weight * pb[k, j].astype(jnp.float32) + jnp.dot(
                direction, dv[:, span(j)], preferred_element_type=jnp.float32
            )

    def dot_up(k):
        total = None
        for j in range(chunks):
            @pl.when(has_after)
            def _():
                up_copy(k, j).wait_recv()

            part = jnp.dot(up[k, j], tv[span(j)], preferred_element_type=jnp.float32)
            total = part if total is None else total + part
        return total

    def coupled(k, j):
        total = 0.0
        for shift in range(1, pops):
            if j == 0:
                anc_copy(k, shift).wait_recv()
            other = lax.rem(pop + pops - shift, pops)
            total = total + prior[pop, other] * anc[k, shift - 1, j].astype(jnp.float32)
        return total

    def turn_next():
        for i in range(length // LANES):
            at = pl.ds(i * LANES, LANES)
            tv[at] = jnp.transpose(nv[:, at])

    def inner(left, right):
        return jnp.sum(left * right, axis=1, keepdims=True)

    for k in range(2):
        if k > 0:
            send_carry(k)
        dot_diag(k)
        if k == 0:
            turn_next()
        image[k] = image[k] + dot_up(k)
        for j in range(chunks):
            both = image[k, :, span(j)] + coupled(k, j)

            @pl.when(has_before)
            def _():
                carry_copy(k, j).wait_recv()

            both = both + carry_in[k, j].astype(jnp.float32)
            image[k, :, span(j)] = both
            following = scale[:, span(j)] * both - p[k, :, span(j)]
            p[k + 1, :, span(j)] = following
            pb[k + 1, j] = following.astype(jnp.bfloat16)
            send_direction(k + 1, j)

    lane_ids = lax.broadcasted_iota(jnp.int32, (traits, LANES), 1)

    def as_rows(columns):
        packed = jnp.zeros((traits, LANES), jnp.float32)
        for j, column in enumerate(columns):
            packed = jnp.where(lane_ids == j, column, packed)
        packed = jnp.concatenate(
            [packed, jnp.zeros((LANES - traits, LANES), jnp.float32)], axis=0
        )
        return jnp.transpose(packed)[:8]

    sums[me] = as_rows([
        inner(p[0], zv[...]), inner(p[1], zv[...]), inner(p[2], zv[...]),
        inner(p[0], image[0]), inner(p[0], image[1]), inner(p[1], image[1]),
        inner(p[2], image[0]), inner(p[2], image[1]),
    ])
    for_each(0, members - 1, lambda k: sums_copy(k).start())

    dot_diag(2)
    other_part = jnp.concatenate([coupled(2, j) for j in range(chunks)], axis=1)
    last = inner(p[2], image[2] + 2.0 * dot_up(2) + other_part)
    tail[me] = as_rows([last])[:1]
    for_each(0, members - 1, lambda k: tail_copy(k).start())

    for_each(1, members, lambda k: arrival(sums, sums_send, sums_recv, k).wait_recv())
    total = jnp.sum(sums[...], axis=0)
    b0, b1, b2, g00, g01, g11, g02, g12 = (total[j : j + 1] for j in range(8))
    l10 = g01 / g00
    d1 = g11 - l10 * g01
    l20 = g02 / g00
    cross = g12 - l20 * g01
    l21 = cross / d1
    y1 = b1 - l10 * b0
    y2 = b2 - l20 * b0 - l21 * y1
    known = l20 * g02 + l21 * cross
    z0 = b0 / g00
    z1 = y1 / d1

    for_each(1, members, lambda k: arrival(tail, tail_send, tail_recv, k).wait_recv())
    g22 = jnp.sum(tail[...], axis=0)
    c2 = y2 / (g22 - known)
    c1 = z1 - l21 * c2
    c0 = z0 - l10 * c1 - l20 * c2
    stacked = jnp.concatenate(
        [c0, c1, c2, jnp.zeros((LANES - 3, LANES), jnp.float32)], axis=0
    )
    stacked = jnp.transpose(stacked)[:traits]
    out_ref[0] = (
        stacked[:, 0:1] * p[0] + stacked[:, 1:2] * p[1] + stacked[:, 2:3] * p[2]
    )

    for k in range(3):
        for j in range(chunks):
            @pl.when(has_before)
            def _():
                up_copy(k, j).wait_send()

        for shift in range(1, pops):
            anc_copy(k, shift).wait_send()
    for k in range(2):
        for j in range(chunks):
            @pl.when(has_after)
            def _():
                carry_copy(k, j).wait_send()
    for_each(0, members - 1, lambda k: sums_copy(k).wait_send())
    for_each(0, members - 1, lambda k: tail_copy(k).wait_send())


def solution(mesh):
    blocks, pops = mesh.shape["genome"], mesh.shape["ancestry"]
    members = blocks * pops

    def body(zscores, ld_diag, ld_next, prior_precision, chrom_cut, band_width):
        _, traits, length = zscores.shape
        bf16, f32 = jnp.bfloat16, jnp.float32
        dma = pltpu.SemaphoreType.DMA
        others = max(pops - 1, 1)
        chunks = length // COLS
        return pl.pallas_call(
            functools.partial(kernel, blocks, pops),
            out_shape=jax.ShapeDtypeStruct(zscores.shape, f32),
            in_specs=[pl.BlockSpec(memory_space=pltpu.HBM)] * 6,
            out_specs=pl.BlockSpec(memory_space=pltpu.VMEM),
            scratch_shapes=[
                pltpu.SMEM(prior_precision.shape, f32),
                pltpu.SMEM(chrom_cut.shape, jnp.int32),
                pltpu.SMEM(band_width.shape, jnp.int32),
                pltpu.VMEM((traits, length), f32),
                pltpu.VMEM((length, length), bf16),
                pltpu.VMEM((length, length), bf16),
                pltpu.VMEM((length, length), bf16),
                pltpu.VMEM((1, length), f32),
                pltpu.VMEM((3, traits, length), f32),
                pltpu.VMEM((3, chunks, traits, COLS), bf16),
                pltpu.VMEM((3, traits, length), f32),
                pltpu.VMEM((3, chunks, traits, COLS), bf16),
                pltpu.VMEM((3, others, chunks, traits, COLS), bf16),
                pltpu.VMEM((2, chunks, traits, COLS), bf16),
                pltpu.VMEM((2, chunks, traits, COLS), bf16),
                pltpu.VMEM((members, 8, LANES), f32),
                pltpu.VMEM((members, 1, LANES), f32),
                dma((4 + 2 * chunks,)),
                dma((3, chunks)), dma((3, chunks)),
                dma((3, others)), dma((3, others)),
                dma((2, chunks)), dma((2, chunks)),
                dma((members,)), dma((members,)), dma((members,)), dma((members,)),
            ],
            compiler_params=pltpu.CompilerParams(
                collective_id=0, has_side_effects=True, vmem_limit_bytes=64 << 20
            ),
        )(prior_precision, chrom_cut, band_width, zscores, ld_diag, ld_next)

    return jax.shard_map(
        body,
        mesh=mesh,
        in_specs=(
            P("ancestry", "trait", ("groups", "genome")),
            P("ancestry", ("groups", "genome"), None),
            P("ancestry", ("groups", "genome"), None),
            P(),
            P("groups"),
            P("groups"),
        ),
        out_specs=P("ancestry", "trait", ("groups", "genome")),
        check_vma=False,
    )
```
